32 devices in a mesh: dp: 4 (over y, core), proto: 8 (over z, x).
Axes of the slice: x: 2, y: 2, z: 4, core: 2. Of those that a mesh axis runs over, the one named last changes fastest.
Arguments:
- student_rows: bfloat16 [64, 256, 256], P('dp'), may hold values from -0.375 to 0.375
- teacher_rows: bfloat16 [64, 256, 256], P('dp'), may hold values from -0.375 to 0.375
- student_proto: bfloat16 [256, 131072], P(None, 'proto'), may hold values from -0.375 to 0.375
- teacher_proto: bfloat16 [256, 131072], P(None, 'proto'), may hold values from -0.375 to 0.375
- center: float32 [131072], P('proto'), may hold values from -0.05 to 0.05
- counts: int32 [64], replicated, may hold values from 1 to 128, 6144 in all
- mask_order: int32 [64, 256], P('dp'), may hold values from 0 to 255, each once within a row
Outputs:
- row_loss: float32 [4, 1536], P('dp')
- student_grad: bfloat16 [4, 1536, 256], P('dp')
The draws below stay inside these ranges and needn't reach their ends.
Inputs may be any that keep to these rules, and one draw needn't show every extreme that they name: counts sum to 6144, and some image has exactly 128. `mask_order`: each row is a permutation of the patch positions; image i's masked patches are its first counts[i] entries.
All inputs are finite; a program needn't handle non-finite values.
Results may differ from the reference program's by a relative error of at most 0.002.
The reference program's roundings to bfloat16 on the way count: a program that leaves them out, or rounds other values in their place, can miss the bound.
Values may be sent and summed in bfloat16 or wider, within the bound.
No kernel may reach another device: no remote copies, remote signals or barrier semaphores. Data moves between devices by JAX's collectives and lax.ppermute only.
A program may use at most 320 MiB of HBM per device.

```python
import math
import jax
import jax.numpy as jnp
import numpy as np
from jax import lax

E = 256
PROTOS = 131072
PATCHES = 256
MASK_IMG = 96
MAXM = 128
IMAGES = 64
MASK_DEV = 1536
N_DP = 4
N_PROTO = 8


def shard_levels(stream_key, shape, split, low, high):
    gain = 1.0
    for axis_at, blocks in split:
        steps = jax.random.uniform(jax.random.fold_in(jax.random.fold_in(stream_key, 6), axis_at), (blocks,), jnp.float32, low / len(split), high / len(split))
        gain = gain * jnp.repeat(jnp.exp(steps), shape[axis_at] // blocks).reshape((-1,) + (1,) * (len(shape) - 1 - axis_at))
    return gain


def profile(count, total, limit, skew):
    loads = [(1 << 20) // math.isqrt(standing ** skew) + 1 for standing in range(2, count + 1)]
    surplus, holding = total - limit - (count - 1), [1] * (count - 1)
    while surplus > 0:
        free = [i for i in range(count - 1) if holding[i] < limit]
        whole, remaining = sum([loads[i] for i in free]), surplus
        for i in free:
            extra = min(limit - holding[i], max(1, remaining * loads[i] // whole), surplus)
            holding[i] = holding[i] + extra
            surplus = surplus - extra
    return np.array([limit] + holding)


def ragged_sizes(own_key, count, total, most, slope):
    if count == 2:
        one = jax.random.randint(own_key, (), max(1, total - most), min(most, total - 1) + 1)
        return jnp.stack([one, total - one])
    tallies = jnp.asarray(profile(count, total, most, slope), jnp.int32)
    twos = (count - 1) // 2
    donor, receiver = tallies[1:1 + 2 * twos:2], tallies[2:2 + 2 * twos:2]
    margin = jnp.minimum(donor - 1, most - receiver)
    moved = jax.random.randint(jax.random.fold_in(own_key, 1), (twos,), 0, 1 << 20) % (margin + 1)
    tallies = tallies.at[1:1 + 2 * twos:2].set(donor - moved).at[2:2 + 2 * twos:2].set(receiver + moved)
    return tallies[jax.random.permutation(jax.random.fold_in(own_key, 2), count)]


def scatter_about(key, shape, scale, most, shards=(), kind=jnp.bfloat16):
    entries = scale * jax.random.normal(key, shape, jnp.float32)
    if shards:
        entries = entries * shard_levels(key, shape, shards, -0.22, 0.18)
    return jnp.clip(entries, -most, most).astype(kind)


def setup_inputs(seed: int = 0) -> dict:
    key_list = jax.random.split(jax.random.key(seed), 8)
    student_rows = scatter_about(key_list[0], (IMAGES, PATCHES, E), 0.0625, 0.375, ((0, 4),))
    teacher_rows = scatter_about(key_list[1], (IMAGES, PATCHES, E), 0.0625, 0.375, ((0, 4),))
    student_proto = scatter_about(key_list[2], (E, PROTOS), E ** -0.5, 0.375, ((1, 8),))
    teacher_proto = scatter_about(key_list[3], (E, PROTOS), E ** -0.5, 0.375, ((1, 8),))
    center = jnp.clip(jax.random.uniform(key_list[4], (PROTOS,), jnp.float32, -0.05, 0.05) * shard_levels(key_list[4], (PROTOS,), ((0, 8),), -0.4, 0.0), -0.05, 0.05)
    counts = ragged_sizes(key_list[5], IMAGES, MASK_IMG * IMAGES, MAXM, 2).astype(jnp.int32)
    mask_order = jax.vmap(lambda own: jax.random.permutation(own, PATCHES))(jax.random.split(key_list[6], IMAGES)).reshape((IMAGES, PATCHES)).astype(jnp.int32)
    return dict(student_rows=student_rows, teacher_rows=teacher_rows, student_proto=student_proto, teacher_proto=teacher_proto, center=center, counts=counts, mask_order=mask_order)


STUDENT_TEMP = 0.1
TEACHER_TEMP = 0.07
EPSILON = 1e-06

def reference(student_rows, teacher_rows, student_proto, teacher_proto, center, counts, mask_order):
    total_rows = MASK_IMG * IMAGES
    image_ends = jnp.cumsum(counts).astype(jnp.int32)
    image_starts = (image_ends - counts).astype(jnp.int32)
    global_pos = jnp.arange(total_rows, dtype=jnp.int32)
    image_ids = lax.optimization_barrier(jnp.sum((global_pos[:, None] >= image_ends[None, :]).astype(jnp.int32), axis=1)).astype(jnp.int32)
    within = (global_pos - image_starts[image_ids]).astype(jnp.int32)
    patch_ids = mask_order[image_ids, within]
    student_in = student_rows[image_ids, patch_ids].astype(jnp.float32)
    teacher_in = teacher_rows[image_ids, patch_ids].astype(jnp.float32)
    student_norm = jnp.sqrt(lax.optimization_barrier(jnp.sum(student_in * student_in, axis=-1, keepdims=True)) + EPSILON)
    teacher_norm = jnp.sqrt(lax.optimization_barrier(jnp.sum(teacher_in * teacher_in, axis=-1, keepdims=True)) + EPSILON)
    student_unit = (student_in / student_norm).astype(jnp.bfloat16)
    teacher_unit = (teacher_in / teacher_norm).astype(jnp.bfloat16)

    def norm_columns(weights):
        wide = weights.astype(jnp.float32)
        return (wide / jnp.sqrt(lax.optimization_barrier(jnp.sum(wide * wide, axis=0, keepdims=True)) + EPSILON)).astype(jnp.bfloat16)
    block_cols = PROTOS // N_PROTO
    student_blocks = norm_columns(student_proto).reshape(E, N_PROTO, block_cols).transpose(1, 0, 2)
    teacher_blocks = norm_columns(teacher_proto).reshape(E, N_PROTO, block_cols).transpose(1, 0, 2)
    center_blocks = center.reshape(N_PROTO, block_cols)

    def exponentials(student_block, teacher_block, center_block):
        student_logit = jnp.dot(student_unit, student_block, preferred_element_type=jnp.float32)
        teacher_logit = jnp.dot(teacher_unit, teacher_block, preferred_element_type=jnp.float32)
        student_exp = jnp.exp(student_logit / STUDENT_TEMP)
        teacher_exp = jnp.exp((teacher_logit - center_block[None, :]) / TEACHER_TEMP)
        return (student_logit, student_exp, teacher_exp)

    def statistic_pass(running, block_in):
        student_logit, student_exp, teacher_exp = exponentials(*block_in)
        return ((running[0] + lax.optimization_barrier(jnp.sum(student_exp, axis=1)), running[1] + lax.optimization_barrier(jnp.sum(teacher_exp, axis=1)), running[2] + lax.optimization_barrier(jnp.sum(teacher_exp * (student_logit / STUDENT_TEMP), axis=1))), None)
    zero_rows = jnp.zeros((total_rows,), jnp.float32)
    sums, unused = lax.scan(statistic_pass, (zero_rows, zero_rows, zero_rows), (student_blocks, teacher_blocks, center_blocks))
    student_sum, teacher_sum, cross_sum = sums
    row_losses = jnp.log(student_sum) - cross_sum / teacher_sum

    def gradient_pass(running, block_in):
        student_logit, student_exp, teacher_exp = exponentials(*block_in)
        logit_grad = ((student_exp / student_sum[:, None] - teacher_exp / teacher_sum[:, None]) / STUDENT_TEMP).astype(jnp.bfloat16)
        term = lax.dot_general(logit_grad, block_in[0], (((1,), (1,)), ((), ())), preferred_element_type=jnp.float32)
        return (running + term, None)
    feature_grad, unused = lax.scan(gradient_pass, jnp.zeros((total_rows, E), jnp.float32), (student_blocks, teacher_blocks, center_blocks))
    inner = lax.optimization_barrier(jnp.sum(student_in * feature_grad, axis=-1, keepdims=True))
    input_grad = feature_grad / student_norm - student_in * inner / (student_norm * student_norm * student_norm)
    row_loss = row_losses.reshape(MASK_DEV, N_DP).T
    student_grad = input_grad.astype(jnp.bfloat16).reshape(MASK_DEV, N_DP, E).transpose(1, 0, 2)
    return (row_loss, student_grad)
```

```python
import functools
import math

import jax
import jax.numpy as jnp
from jax import lax
from jax.experimental import pallas as pl
from jax.experimental.pallas import tpu as pltpu
from jax.sharding import PartitionSpec as P

MASK_IMG = 96
STUDENT_TEMP = 0.1
TEACHER_TEMP = 0.07
EPSILON = 1e-06
LOG2E = math.log2(math.e)
STUDENT_GAIN = LOG2E / STUDENT_TEMP
TEACHER_GAIN = LOG2E / TEACHER_TEMP
WIRE_GAIN = 1024.0
LANES = 128
ROW_BLOCK = 256
PASS1_COLS = 1024
PASS2_COLS = 1024
VMEM_BYTES = 60 * 1024 * 1024
F32 = jnp.float32
BF16 = jnp.bfloat16


def params():
    return pltpu.CompilerParams(
        dimension_semantics=("arbitrary",), vmem_limit_bytes=VMEM_BYTES
    )


def whole(shape):
    return pl.BlockSpec(shape, lambda i, *_: (0,) * len(shape))


def prep_kernel(
    dp_count, scalars, student, teacher, order, xs_out, zs_out, zt_out, inv_out, xs_all, xt_all
):
    image = pl.program_id(0)
    images = pl.num_programs(0)
    patches = student.shape[1]
    most = patches // 2

    @pl.when(image == 0)
    def _():
        xs_all[...] = jnp.zeros_like(xs_all)
        xt_all[...] = jnp.zeros_like(xt_all)

    start = scalars[image]
    base, shift = pl.multiple_of(start // 8 * 8, 8), lax.rem(start, 8)
    lane = lax.broadcasted_iota(jnp.int32, (8, patches), 1)
    listed = jnp.broadcast_to(order[pl.ds(image, 1), :], (8, patches))
    listed = jnp.where(lane < scalars[images + image], listed, -1)
    listed = pltpu.roll(listed, shift, 1)[0:1, :]
    patch = lax.broadcasted_iota(jnp.int32, (patches, patches), 0)
    chosen = jnp.where(patch == jnp.broadcast_to(listed, (patches, patches)), 1.0, 0.0).astype(BF16)
    dims = (((0,), (0,)), ((), ()))
    for rows, kept in ((student, xs_all), (teacher, xt_all)):
        picked = lax.dot_general(chosen, rows[0], dims, preferred_element_type=F32)
        for half in range(kept.shape[0]):
            kept[half, pl.ds(base, most + 8), :] += picked[
                : most + 8, half * LANES : (half + 1) * LANES
            ]

    @pl.when(image == images - 1)
    def _():
        phase = scalars[2 * images]
        group = LANES // dp_count

        @pl.loop(0, xs_out.shape[0] // LANES)
        def _(block):
            first = block * LANES
            norms = []
            for rank in range(dp_count):
                lead = lax.rem(rank + dp_count - phase, dp_count)
                rows = pl.ds(first + lead, group, stride=dp_count)
                out = pl.ds(pl.multiple_of(first + rank * group, group), group)
                halves = range(xs_all.shape[0])
                student_in = jnp.concatenate([xs_all[h, rows, :] for h in halves], axis=1)
                teacher_in = jnp.concatenate([xt_all[h, rows, :] for h in halves], axis=1)
                student_norm = jnp.sqrt(
                    jnp.sum(student_in * student_in, axis=1, keepdims=True) + EPSILON
                )
                teacher_norm = jnp.sqrt(
                    jnp.sum(teacher_in * teacher_in, axis=1, keepdims=True) + EPSILON
                )
                xs_out[out, :] = student_in.astype(BF16)
                zs_out[out, :] = (student_in / student_norm).astype(BF16)
                zt_out[out, :] = (teacher_in / teacher_norm).astype(BF16)
                norms.append(1.0 / student_norm)
            column = jnp.concatenate(norms, axis=0)
            inv_out[pl.ds(block, 1), :] = jnp.broadcast_to(column, (LANES, LANES)).T[0:1, :]


def prep(scalars, student_rows, teacher_rows, mask_order, dp_count):
    images, patches, width = student_rows.shape
    rows = images * (patches // 2)
    padded = rows + patches // 2
    image_block = pl.BlockSpec((1, patches, width), lambda i, *_: (i, 0, 0))
    return pl.pallas_call(
        functools.partial(prep_kernel, dp_count),
        out_shape=[
            jax.ShapeDtypeStruct((rows, width), BF16),
            jax.ShapeDtypeStruct((rows, width), BF16),
            jax.ShapeDtypeStruct((rows, width), BF16),
            jax.ShapeDtypeStruct((rows // LANES, LANES), F32),
        ],
        grid_spec=pltpu.PrefetchScalarGridSpec(
            num_scalar_prefetch=1,
            grid=(images,),
            in_specs=[image_block, image_block, whole(mask_order.shape)],
            out_specs=[
                whole((rows, width)),
                whole((rows, width)),
                whole((rows, width)),
                whole((rows // LANES, LANES)),
            ],
            scratch_shapes=[pltpu.VMEM((width // LANES, padded, LANES), F32)] * 2,
        ),
        compiler_params=params(),
        name="prep",
    )(scalars, student_rows, teacher_rows, mask_order)


def unit_columns(block):
    wide = block.astype(F32)
    return (wide * (1.0 / jnp.sqrt(jnp.sum(wide * wide, axis=0, keepdims=True) + EPSILON))).astype(
        BF16
    )


def row_blocks(used, first, total):
    blocks = (used - first + ROW_BLOCK - 1) // ROW_BLOCK
    return jnp.clip(blocks, 0, total // ROW_BLOCK)


def sums_kernel(first_row, raw, scalars, zs, zt, student, teacher, center, *refs):
    if raw:
        sums_out, ws, wt, es_acc, et_acc, cross_acc = refs
        ws[...] = unit_columns(student[...])
        wt[...] = unit_columns(teacher[...])
    else:
        sums_out, es_acc, et_acc, cross_acc = refs
        ws, wt = student, teacher
    step = pl.program_id(0)

    @pl.when(step == 0)
    def _():
        es_acc[...] = jnp.zeros_like(es_acc)
        et_acc[...] = jnp.zeros_like(et_acc)
        cross_acc[...] = jnp.zeros_like(cross_acc)

    cols = ws.shape[1]

    def body(block, carry):
        at = pl.ds(pl.multiple_of(block * ROW_BLOCK, ROW_BLOCK), ROW_BLOCK)
        s = jnp.dot(zs[at, :], ws[...], preferred_element_type=F32)
        t = jnp.dot(zt[at, :], wt[...], preferred_element_type=F32)
        es_sum, et_sum, cross_sum = es_acc[at, :], et_acc[at, :], cross_acc[at, :]
        for c in range(0, cols, LANES):
            s_part = s[:, c : c + LANES] * STUDENT_GAIN
            es_sum += jnp.exp2(s_part)
            et = jnp.exp2(
                t[:, c : c + LANES] * TEACHER_GAIN - center[:, c : c + LANES] * TEACHER_GAIN
            )
            et_sum += et
            cross_sum += et * s_part
        es_acc[at, :], et_acc[at, :], cross_acc[at, :] = es_sum, et_sum, cross_sum
        return carry

    lax.fori_loop(0, row_blocks(scalars[0], first_row, es_acc.shape[0]), body, 0)

    @pl.when(step == pl.num_programs(0) - 1)
    def _():
        for k, acc in enumerate((es_acc, et_acc, cross_acc)):
            for block in range(es_acc.shape[0] // LANES):
                tile = acc[block * LANES : (block + 1) * LANES, :].T
                sums_out[k, block : block + 1, :] = jnp.sum(tile, axis=0, keepdims=True)


def sums(scalars, zs, zt, student, teacher, center, first_row, rows, raw):
    width, protos = student.shape
    cols = min(PASS1_COLS, protos)
    rows_block = pl.BlockSpec((pl.Element(rows), pl.Element(width)), lambda i, *_: (first_row, 0))
    col_block = pl.BlockSpec((width, cols), lambda i, *_: (0, i))
    outs = [jax.ShapeDtypeStruct((3, rows // LANES, LANES), F32)]
    specs = [whole((3, rows // LANES, LANES))]
    if raw:
        outs += [jax.ShapeDtypeStruct((width, protos), BF16)] * 2
        specs += [col_block] * 2
    out = pl.pallas_call(
        functools.partial(sums_kernel, first_row, raw),
        out_shape=outs,
        grid_spec=pltpu.PrefetchScalarGridSpec(
            num_scalar_prefetch=1,
            grid=(protos // cols,),
            in_specs=[
                rows_block,
                rows_block,
                col_block,
                col_block,
                pl.BlockSpec((1, cols), lambda i, *_: (0, i)),
            ],
            out_specs=specs,
            scratch_shapes=[pltpu.VMEM((rows, LANES), F32)] * 3,
        ),
        compiler_params=params(),
        cost_estimate=pl.CostEstimate(
            flops=4 * rows * width * protos,
            bytes_accessed=8 * width * protos,
            transcendentals=2 * rows * protos,
        ),
        name="sums",
    )(scalars, zs, zt, student, teacher, center)
    return out if raw else (out[0], student, teacher)


def grad_kernel(
    first_row, dp_count, scalars, zs, zt, xs, totals, ws, wt, center, out, es_gain, et_gain, dz_acc
):
    step = pl.program_id(0)
    rows = dz_acc.shape[0]

    @pl.when(step == 0)
    def _():
        dz_acc[...] = jnp.zeros_like(dz_acc)
        for k, gain in enumerate((es_gain, et_gain)):
            for block in range(rows // LANES):
                line = (1.0 / STUDENT_TEMP) / totals[k, block : block + 1, :]
                gain[block * LANES : (block + 1) * LANES, :] = jnp.broadcast_to(
                    line, (LANES, LANES)
                ).T

    cols = ws.shape[1]

    def body(block, carry):
        at = pl.ds(pl.multiple_of(block * ROW_BLOCK, ROW_BLOCK), ROW_BLOCK)
        s = jnp.dot(zs[at, :], ws[...], preferred_element_type=F32)
        t = jnp.dot(zt[at, :], wt[...], preferred_element_type=F32)
        es_scale, et_scale = es_gain[at, :], et_gain[at, :]
        parts = []
        for c in range(0, cols, LANES):
            es = jnp.exp2(s[:, c : c + LANES] * STUDENT_GAIN)
            et = jnp.exp2(
                t[:, c : c + LANES] * TEACHER_GAIN - center[:, c : c + LANES] * TEACHER_GAIN
            )
            parts.append((es * es_scale - et * et_scale).astype(BF16))
        dlogit = jnp.concatenate(parts, axis=1)
        dz_acc[at, :] += lax.dot_general(
            dlogit, ws[...], (((1,), (1,)), ((), ())), preferred_element_type=F32
        )
        return carry

    lax.fori_loop(0, row_blocks(scalars[0], first_row, rows), body, 0)

    @pl.when(step == pl.num_programs(0) - 1)
    def _():
        group = LANES // dp_count
        for block in range(rows // LANES):
            at = slice(block * LANES, (block + 1) * LANES)
            x = xs[at, :].astype(F32)
            dz = dz_acc[at, :]
            square = jnp.sum(x * x, axis=1, keepdims=True) + EPSILON
            inner = jnp.sum(x * dz, axis=1, keepdims=True)
            part = ((dz - x * (inner / square)) * WIRE_GAIN).astype(out.dtype)
            for rank in range(dp_count):
                out[rank, block * group : (block + 1) * group, :] = part[
                    rank * group : (rank + 1) * group, :
                ]


def grads(scalars, zs, zt, xs, totals, ws, wt, center, first_row, rows, dp_count):
    width, protos = ws.shape
    cols = min(PASS2_COLS, protos)
    rows_block = pl.BlockSpec((pl.Element(rows), pl.Element(width)), lambda i, *_: (first_row, 0))
    col_block = pl.BlockSpec((width, cols), lambda i, *_: (0, i))
    return pl.pallas_call(
        functools.partial(grad_kernel, first_row, dp_count),
        out_shape=jax.ShapeDtypeStruct((dp_count, rows // dp_count, width), F32),
        grid_spec=pltpu.PrefetchScalarGridSpec(
            num_scalar_prefetch=1,
            grid=(protos // cols,),
            in_specs=[
                rows_block,
                rows_block,
                rows_block,
                whole(totals.shape),
                col_block,
                col_block,
                pl.BlockSpec((1, cols), lambda i, *_: (0, i)),
            ],
            out_specs=whole((dp_count, rows // dp_count, width)),
            scratch_shapes=[
                pltpu.VMEM((rows, LANES), F32),
                pltpu.VMEM((rows, LANES), F32),
                pltpu.VMEM((rows, width), F32),
            ],
        ),
        compiler_params=params(),
        cost_estimate=pl.CostEstimate(
            flops=6 * rows * width * protos,
            bytes_accessed=4 * width * protos,
            transcendentals=2 * rows * protos,
        ),
        name="grads",
    )(scalars, zs, zt, xs, totals, ws, wt, center)


def place_kernel(scalars, *refs):
    *pieces, out, stage = refs
    sources = pieces[0].shape[0]
    stage[...] = jnp.zeros_like(stage)
    to = lax.broadcasted_iota(jnp.int32, (LANES + 8, LANES), 0)
    of = lax.broadcasted_iota(jnp.int32, (LANES + 8, LANES), 1)
    for source in range(sources):
        offset, left = scalars[source], scalars[source + 1] - scalars[source]
        base, shift = pl.multiple_of(offset // 8 * 8, 8), lax.rem(offset, 8)
        done = 0
        for piece in pieces:
            for at in range(0, piece.shape[1], LANES):
                length = min(LANES, piece.shape[1] - at)
                moved = (to[: length + 8, :length] == of[: length + 8, :length] + shift) & (
                    of[: length + 8, :length] < left - done
                )

                @pl.when(left > done)
                def _():
                    stage[pl.ds(base + done, length + 8), :] += jnp.dot(
                        jnp.where(moved, 1.0, 0.0).astype(BF16),
                        piece[source, at : at + length, :],
                        preferred_element_type=F32,
                    )

                done += length
    out[0] = stage[0 : out.shape[1], :].astype(out.dtype)


def place(scalars, pieces, mask_dev):
    width = pieces[0].shape[2]
    return pl.pallas_call(
        place_kernel,
        out_shape=jax.ShapeDtypeStruct((1, mask_dev, width), BF16),
        grid_spec=pltpu.PrefetchScalarGridSpec(
            num_scalar_prefetch=1,
            grid=(1,),
            in_specs=[whole(p.shape) for p in pieces],
            out_specs=whole((1, mask_dev, width)),
            scratch_shapes=[pltpu.VMEM((mask_dev + LANES + 8, width), F32)],
        ),
        compiler_params=params(),
        name="place",
    )(scalars, *pieces)


def local(student_rows, teacher_rows, student_proto, teacher_proto, center, counts, mask_order):
    img_dev, patches, width = student_rows.shape
    dp_count, proto_count = lax.axis_size("dp"), lax.axis_size("proto")
    dp_index = lax.axis_index("dp")
    rows = img_dev * (patches // 2)
    mask_dev = MASK_IMG * img_dev
    per_dev = counts.reshape(dp_count, img_dev)
    dev_counts = jnp.sum(per_dev, axis=1)
    dev_ends = jnp.cumsum(dev_counts)
    dev_starts = dev_ends - dev_counts
    own = lax.dynamic_slice_in_dim(per_dev, dp_index, 1, axis=0)[0]
    own_start = lax.dynamic_slice_in_dim(dev_starts, dp_index, 1)
    prep_scalars = jnp.concatenate(
        [jnp.cumsum(own) - own, own, lax.rem(own_start, dp_count)]
    ).astype(jnp.int32)
    own_count = jnp.sum(own).astype(jnp.int32)[None]
    first_rows = (dev_starts - dp_index + dp_count - 1) // dp_count

    xs, zs, zt, inv = prep(prep_scalars, student_rows, teacher_rows, mask_order, dp_count)
    center_row = center[None, :]
    part, ws, wt = sums(
        own_count, zs, zt, student_proto, teacher_proto, center_row, 0, rows, True
    )
    everyone = lax.all_to_all(
        jnp.broadcast_to(part[None], (proto_count,) + part.shape), "proto", 0, 0, tiled=True
    )
    totals = jnp.sum(everyone, axis=0)
    safe = jnp.where(totals[:2] > 0, totals[:2], 1.0)
    loss = jnp.log(safe[0]) - totals[2] / safe[1] / LOG2E
    dz = grads(own_count, zs, zt, xs, safe, ws, wt, center_row, 0, rows, dp_count)

    side = jnp.stack([loss, inv])
    sides = lax.all_to_all(
        jnp.broadcast_to(side[None], (dp_count,) + side.shape), "dp", 0, 0, tiled=True
    )
    group = LANES // dp_count
    mine = lax.dynamic_slice_in_dim(
        sides.reshape(dp_count, 2, rows // LANES, dp_count, group), dp_index, 1, axis=3
    ).reshape(dp_count, 2, rows // dp_count)
    share = rows // dp_count // proto_count
    wire = dz.astype(jnp.float16).reshape(dp_count * proto_count, share, width)
    got = lax.all_to_all(wire, ("dp", "proto"), 0, 0, tiled=True)
    summed = jnp.sum(
        got.reshape(dp_count, proto_count, share, width).astype(F32), axis=1
    ) * (1.0 / WIRE_GAIN)
    proto_index = lax.axis_index("proto")
    inv_mine = lax.dynamic_slice_in_dim(mine[:, 1], proto_index * share, share, axis=1)
    dx = (summed * inv_mine[..., None]).astype(BF16)
    gathered = lax.all_to_all(
        jnp.broadcast_to(dx[None], (proto_count,) + dx.shape), "proto", 0, 0, tiled=True
    )
    piece = gathered.transpose(1, 0, 2, 3).reshape(dp_count, rows // dp_count, width)
    bounds = jnp.concatenate([first_rows, jnp.full((1,), mask_dev)]).astype(jnp.int32)
    student_grad = place(bounds, [piece], mask_dev)

    position = jnp.arange(mask_dev, dtype=jnp.int32)
    source = jnp.sum(
        (position[:, None] >= first_rows[None, :]).astype(jnp.int32), axis=1
    ) - 1
    index = source * (rows // dp_count) + position - jnp.take(first_rows, source)
    row_loss = jnp.take(mine[:, 0].reshape(-1), index)
    return (row_loss[None, :], student_grad)


def solution(mesh):
    placed = (
        P("dp", None, None),
        P("dp", None, None),
        P(None, "proto"),
        P(None, "proto"),
        P("proto"),
        P(),
        P("dp", None),
    )
    return jax.shard_map(
        local,
        mesh=mesh,
        in_specs=placed,
        out_specs=(P("dp", None), P("dp", None, None)),
        check_vma=False,
    )
```

```python
import functools
import math

import jax
import jax.numpy as jnp
from jax import lax
from jax.experimental import pallas as pl
from jax.experimental.pallas import tpu as pltpu
from jax.sharding import PartitionSpec as P

MASK_IMG = 96
STUDENT_TEMP = 0.1
TEACHER_TEMP = 0.07
EPSILON = 1e-06
LOG2E = math.log2(math.e)
STUDENT_GAIN = LOG2E / STUDENT_TEMP
TEACHER_GAIN = LOG2E / TEACHER_TEMP
WIRE_GAIN = 1024.0
LANES = 128
SUM_ROWS = 608
COL_TILE = 256
PASS1_COLS = 1024
PASS2_COLS = 512
VMEM_BYTES = 60 * 1024 * 1024
F32 = jnp.float32
BF16 = jnp.bfloat16
WIRE = jnp.float16


def params():
    return pltpu.CompilerParams(
        dimension_semantics=("arbitrary",), vmem_limit_bytes=VMEM_BYTES
    )


def whole(shape):
    return pl.BlockSpec(shape, lambda i, *_: (0,) * len(shape))


def own_sum(scalars, images, limit):
    return lax.fori_loop(0, limit, lambda i, total: total + scalars[i], jnp.int32(0))


def prep_kernel(
    dp_count, scalars, student, teacher, order, xs_out, zs_out, zt_out, inv_out, xs_all, xt_all, fill
):
    image = pl.program_id(0)
    images = pl.num_programs(0)
    patches = student.shape[1]
    most = patches // 2
    first_image = scalars[images * dp_count] * images

    @pl.when(image == 0)
    def _():
        xs_all[...] = jnp.zeros_like(xs_all)
        xt_all[...] = jnp.zeros_like(xt_all)
        fill[0] = 0

    start, count = fill[0], scalars[first_image + image]
    fill[0] = start + count
    base = pl.multiple_of(lax.div(start, 8) * 8, 8)
    shift = lax.rem(start, 8)
    lane = lax.broadcasted_iota(jnp.int32, (8, patches), 1)
    listed = jnp.broadcast_to(order[pl.ds(image, 1), :], (8, patches))
    listed = pltpu.roll(jnp.where(lane < count, listed, -1), shift, 1)
    column = listed.astype(F32).T[: most + 16, 0:1]
    patch = lax.broadcasted_iota(jnp.int32, (most + 16, patches), 1).astype(F32)
    chosen = jnp.where(patch == jnp.broadcast_to(column, patch.shape), 1.0, 0.0).astype(BF16)
    for rows, kept in ((student, xs_all), (teacher, xt_all)):
        picked = jnp.dot(chosen, rows[0], preferred_element_type=F32)
        for half in range(kept.shape[0]):
            kept[half, pl.ds(base, most + 8), :] += picked[
                : most + 8, half * LANES : (half + 1) * LANES
            ]

    @pl.when(image == images - 1)
    def _():
        phase = lax.rem(own_sum(scalars, images, first_image), dp_count)
        group = LANES // dp_count
        used = images * most
        for out in (zs_out, zt_out):
            out[used:, :] = jnp.zeros((out.shape[0] - used, out.shape[1]), out.dtype)

        @pl.loop(0, used // LANES)
        def _(block):
            first = block * LANES
            norms = []
            for rank in range(dp_count):
                lead = lax.rem(rank + dp_count - phase, dp_count)
                rows = pl.ds(first + lead, group, stride=dp_count)
                out = pl.ds(pl.multiple_of(first + rank * group, group), group)
                halves = range(xs_all.shape[0])
                student_in = jnp.concatenate([xs_all[h, rows, :] for h in halves], axis=1)
                teacher_in = jnp.concatenate([xt_all[h, rows, :] for h in halves], axis=1)
                student_norm = jnp.sqrt(
                    jnp.sum(student_in * student_in, axis=1, keepdims=True) + EPSILON
                )
                teacher_norm = jnp.sqrt(
                    jnp.sum(teacher_in * teacher_in, axis=1, keepdims=True) + EPSILON
                )
                xs_out[out, :] = student_in.astype(BF16)
                zs_out[out, :] = (student_in / student_norm).astype(BF16)
                zt_out[out, :] = (teacher_in / teacher_norm).astype(BF16)
                norms.append(1.0 / student_norm)
            column = jnp.concatenate(norms, axis=0)
            inv_out[pl.ds(block, 1), :] = jnp.broadcast_to(column, (LANES, LANES)).T[0:1, :]


def prep(scalars, student_rows, teacher_rows, mask_order, dp_count):
    images, patches, width = student_rows.shape
    rows = images * (patches // 2)
    padded = rows + rows // 4
    image_block = pl.BlockSpec((1, patches, width), lambda i, *_: (i, 0, 0))
    return pl.pallas_call(
        functools.partial(prep_kernel, dp_count),
        out_shape=[
            jax.ShapeDtypeStruct((rows, width), BF16),
            jax.ShapeDtypeStruct((padded, width), BF16),
            jax.ShapeDtypeStruct((padded, width), BF16),
            jax.ShapeDtypeStruct((rows // LANES, LANES), F32),
        ],
        grid_spec=pltpu.PrefetchScalarGridSpec(
            num_scalar_prefetch=1,
            grid=(images,),
            in_specs=[image_block, image_block, whole(mask_order.shape)],
            out_specs=[
                whole((rows, width)),
                whole((padded, width)),
                whole((padded, width)),
                whole((rows // LANES, LANES)),
            ],
            scratch_shapes=[pltpu.VMEM((width // LANES, rows + patches // 2, LANES), F32)] * 2
            + [pltpu.SMEM((1,), jnp.int32)],
        ),
        compiler_params=params(),
        name="prep",
    )(scalars, student_rows, teacher_rows, mask_order)


def unit_columns(block):
    wide = block.astype(F32)
    return (wide * (1.0 / jnp.sqrt(jnp.sum(wide * wide, axis=0, keepdims=True) + EPSILON))).astype(
        BF16
    )


def row_blocks(scalars, dp_count, first, size, most):
    images = (scalars.shape[0] - 1) // dp_count
    start = scalars[images * dp_count] * images
    used = lax.fori_loop(
        0, images, lambda i, total: total + scalars[start + i], jnp.int32(0)
    )
    used = lax.div(used + (LANES - 1), LANES) * LANES
    return jnp.clip(lax.div(used - first + (size - 1), size), 1, most)


def rows_at(size, block):
    return pl.ds(pl.multiple_of(block * size, size), size)


def round_up(rows, size):
    return (rows + size - 1) // size * size


def sums_kernel(dp_count, raw, scalars, zs, zt, student, teacher, center, *refs):
    if raw:
        sums_out, ws, wt, es_acc, et_acc, cross_acc, s_held, t_held = refs
    else:
        sums_out, es_acc, et_acc, cross_acc, s_held, t_held = refs
        ws, wt = student, teacher
    step, last = pl.program_id(0), pl.num_programs(0) - 1
    cols = ws.shape[1]
    blocks = row_blocks(scalars, dp_count, 0, SUM_ROWS, es_acc.shape[0] // SUM_ROWS)

    @pl.when(step == 0)
    def _():
        es_acc[...] = jnp.zeros_like(es_acc)
        et_acc[...] = jnp.zeros_like(et_acc)
        cross_acc[...] = jnp.zeros_like(cross_acc)
        s_held[...] = jnp.full_like(s_held, -1e30)
        t_held[...] = jnp.full_like(t_held, -1e30)

    if raw:

        @pl.when(step < last)
        def _():
            ws[...] = unit_columns(student[...])
            wt[...] = unit_columns(teacher[...])

    def body(block, carry):
        before = jnp.where(block == 0, blocks - 1, block - 1)
        col = jnp.maximum(jnp.where(block == 0, step - 1, step), 0)
        first = pl.multiple_of(before * SUM_ROWS, SUM_ROWS)
        for tile in range(0, cols, COL_TILE):
            shifts = center[:, pl.ds(pl.multiple_of(col * cols + tile, COL_TILE), COL_TILE)] * TEACHER_GAIN
            for sub in range(0, SUM_ROWS, SUM_ROWS):
                at = pl.ds(first + sub, SUM_ROWS)
                here = slice(sub, sub + SUM_ROWS)
                es_sum, et_sum, cross = es_acc[at, :], et_acc[at, :], cross_acc[at, :]
                for c in range(tile, tile + COL_TILE, LANES):
                    shift = shifts[:, c - tile : c - tile + LANES]
                    s = s_held[here, c : c + LANES]
                    es_sum += jnp.exp2(s * STUDENT_GAIN)
                    et = jnp.exp2(t_held[here, c : c + LANES] * TEACHER_GAIN - shift)
                    et_sum += et
                    cross += et * s
                es_acc[at, :], et_acc[at, :], cross_acc[at, :] = es_sum, et_sum, cross
        s_held[...] = jnp.dot(zs[rows_at(SUM_ROWS, block), :], ws[...], preferred_element_type=F32)
        t_held[...] = jnp.dot(zt[rows_at(SUM_ROWS, block), :], wt[...], preferred_element_type=F32)
        return carry

    lax.fori_loop(0, jnp.where(step == last, 1, blocks), body, 0)

    @pl.when(step == last)
    def _():
        for k, acc in enumerate((es_acc, et_acc, cross_acc)):
            for block in range(sums_out.shape[1]):
                tile = acc[block * LANES : (block + 1) * LANES, :].T
                sums_out[k, block : block + 1, :] = jnp.sum(tile, axis=0, keepdims=True)


def sums(scalars, zs, zt, student, teacher, center, mask_rows, dp_count, raw):
    width, protos = student.shape
    rows, padded = mask_rows, round_up(mask_rows, SUM_ROWS)
    cols = min(PASS1_COLS, protos)
    steps = protos // cols
    col_block = pl.BlockSpec((width, cols), lambda i, *_: (0, jnp.minimum(i, steps - 1)))
    outs = [jax.ShapeDtypeStruct((3, rows // LANES, LANES), F32)]
    specs = [whole((3, rows // LANES, LANES))]
    if raw:
        outs += [jax.ShapeDtypeStruct((width, protos), BF16)] * 2
        specs += [col_block] * 2
    out = pl.pallas_call(
        functools.partial(sums_kernel, dp_count, raw),
        out_shape=outs,
        grid_spec=pltpu.PrefetchScalarGridSpec(
            num_scalar_prefetch=1,
            grid=(steps + 1,),
            in_specs=[
                whole(zs.shape),
                whole(zs.shape),
                col_block,
                col_block,
                whole((1, protos)),
            ],
            out_specs=specs,
            scratch_shapes=[pltpu.VMEM((padded, LANES), F32)] * 3
            + [pltpu.VMEM((SUM_ROWS, cols), F32)] * 2,
        ),
        compiler_params=params(),
        cost_estimate=pl.CostEstimate(
            flops=4 * rows * width * protos,
            bytes_accessed=8 * width * protos,
            transcendentals=2 * rows * protos,
        ),
        name="sums",
    )(scalars, zs, zt, student, teacher, center)
    return out if raw else (out[0], student, teacher)


def grad_kernel(
    dp_count,
    first_row,
    size,
    scalars,
    zs,
    zt,
    xs,
    totals,
    ws_before,
    ws,
    wt,
    center,
    out,
    es_gain,
    et_gain,
    dz_acc,
    s_held,
    t_held,
):
    step, last = pl.program_id(0), pl.num_programs(0) - 1
    rows = out.shape[0] * out.shape[1]
    cols = ws.shape[1]
    blocks = row_blocks(scalars, dp_count, first_row, size, dz_acc.shape[0] // size)

    @pl.when(step == 0)
    def _():
        dz_acc[...] = jnp.zeros_like(dz_acc)
        s_held[...] = jnp.full_like(s_held, -1e30)
        t_held[...] = jnp.full_like(t_held, -1e30)
        for k, gain in enumerate((es_gain, et_gain)):
            for block in range(rows // LANES):
                line = (1.0 / STUDENT_TEMP) / totals[k, block : block + 1, :]
                gain[block * LANES : (block + 1) * LANES, :] = jnp.broadcast_to(
                    line, (LANES, LANES)
                ).T

    def consume(half, col, slot, columns):
        at = rows_at(size // 2, half)
        es_scale, et_scale = es_gain[at, :], et_gain[at, :]
        shifts = center[:, pl.ds(pl.multiple_of(col * cols, cols), cols)] * TEACHER_GAIN
        parts = []
        for c in range(0, cols, LANES):
            s = s_held[slot, :, c : c + LANES]
            es = jnp.exp2(s * STUDENT_GAIN) * es_scale
            et = (
                jnp.exp2(t_held[slot, :, c : c + LANES] * TEACHER_GAIN - shifts[:, c : c + LANES])
                * et_scale
            )
            parts.append((es - et).astype(BF16))
        dz_acc[at, :] += lax.dot_general(
            jnp.concatenate(parts, axis=1),
            columns[...],
            (((1,), (1,)), ((), ())),
            preferred_element_type=F32,
        )

    def produce(half, slot):
        s_held[slot] = jnp.dot(zs[rows_at(size // 2, half), :], ws[...], preferred_element_type=F32)
        t_held[slot] = jnp.dot(zt[rows_at(size // 2, half), :], wt[...], preferred_element_type=F32)

    def turn(block, half_before, col_before, columns_before):
        produce(2 * block, 0)
        consume(half_before, col_before, 1, columns_before)
        produce(2 * block + 1, 1)
        consume(2 * block, step, 0, ws)

    def body(block, carry):
        turn(block, 2 * block - 1, step, ws)
        return carry

    col_before = jnp.maximum(step - 1, 0)

    @pl.when(step < last)
    def _():
        turn(0, 2 * blocks - 1, col_before, ws_before)
        lax.fori_loop(1, blocks, body, 0)

    @pl.when(step == last)
    def _():
        consume(2 * blocks - 1, col_before, 1, ws_before)

    @pl.when(step == last)
    def _():
        group = LANES // dp_count
        for block in range(rows // LANES):
            at = slice(block * LANES, (block + 1) * LANES)
            x = xs[at, :].astype(F32)
            dz = dz_acc[at, :]
            square = jnp.sum(x * x, axis=1, keepdims=True) + EPSILON
            inner = jnp.sum(x * dz, axis=1, keepdims=True)
            part = (dz - x * (inner / square)) * WIRE_GAIN
            for rank in range(dp_count):
                out[rank, block * group : (block + 1) * group, :] = part[
                    rank * group : (rank + 1) * group, :
                ].astype(out.dtype)


def grads(scalars, zs, zt, xs, totals, ws, wt, center, first_row, rows, size, dp_count):
    width, protos = ws.shape
    padded = round_up(rows, size)
    part = lambda count, cols: pl.BlockSpec(
        (pl.Element(count), pl.Element(cols)), lambda i, *_: (first_row, 0)
    )
    cols = min(PASS2_COLS, protos)
    steps = protos // cols
    col_block = pl.BlockSpec((width, cols), lambda i, *_: (0, jnp.minimum(i, steps - 1)))
    return pl.pallas_call(
        functools.partial(grad_kernel, dp_count, first_row, size),
        out_shape=jax.ShapeDtypeStruct((dp_count, rows // dp_count, width), F32),
        grid_spec=pltpu.PrefetchScalarGridSpec(
            num_scalar_prefetch=1,
            grid=(steps + 1,),
            in_specs=[
                part(padded, width),
                part(padded, width),
                part(rows, width),
                whole(totals.shape),
                pl.BlockSpec((width, cols), lambda i, *_: (0, jnp.maximum(i - 1, 0))),
                col_block,
                col_block,
                whole((1, protos)),
            ],
            out_specs=whole((dp_count, rows // dp_count, width)),
            scratch_shapes=[pltpu.VMEM((padded, LANES), F32)] * 2
            + [pltpu.VMEM((padded, width), F32)]
            + [pltpu.VMEM((2, size // 2, cols), F32)] * 2,
        ),
        compiler_params=params(),
        cost_estimate=pl.CostEstimate(
            flops=6 * rows * width * protos,
            bytes_accessed=4 * width * protos,
            transcendentals=2 * rows * protos,
        ),
        name=f"grads_{first_row}",
    )(scalars, zs, zt, xs, totals, ws, ws, wt, center)


def place_kernel(scalars, *refs):
    *pieces, out, stage = refs
    sources = pieces[0].shape[0]
    stage[...] = jnp.zeros_like(stage)
    to = lax.broadcasted_iota(jnp.int32, (LANES + 8, LANES), 0)
    of = lax.broadcasted_iota(jnp.int32, (LANES + 8, LANES), 1)
    for source in range(sources):
        offset, left = scalars[source], scalars[source + 1] - scalars[source]
        base, shift = pl.multiple_of(offset // 8 * 8, 8), lax.rem(offset, 8)
        done = 0
        for piece in pieces:
            for at in range(0, piece.shape[1], LANES):
                length = min(LANES, piece.shape[1] - at)
                moved = (to[: length + 8, :length] == of[: length + 8, :length] + shift) & (
                    of[: length + 8, :length] < left - done
                )

                @pl.when(left > done)
                def _():
                    stage[pl.ds(base + done, length + 8), :] += jnp.dot(
                        jnp.where(moved, 1.0, 0.0).astype(BF16),
                        piece[source, at : at + length, :],
                        preferred_element_type=F32,
                    )

                done += length
    out[0] = stage[0 : out.shape[1], :].astype(out.dtype)


def place(scalars, pieces, mask_dev):
    width = pieces[0].shape[2]
    return pl.pallas_call(
        place_kernel,
        out_shape=jax.ShapeDtypeStruct((1, mask_dev, width), BF16),
        grid_spec=pltpu.PrefetchScalarGridSpec(
            num_scalar_prefetch=1,
            grid=(1,),
            in_specs=[whole(p.shape) for p in pieces],
            out_specs=whole((1, mask_dev, width)),
            scratch_shapes=[pltpu.VMEM((mask_dev + LANES + 8, width), F32)],
        ),
        compiler_params=params(),
        name="place",
    )(scalars, *pieces)


def local(student_rows, teacher_rows, student_proto, teacher_proto, center, counts, mask_order):
    img_dev, patches, width = student_rows.shape
    dp_count, proto_count = lax.axis_size("dp"), lax.axis_size("proto")
    dp_index, proto_index = lax.axis_index("dp"), lax.axis_index("proto")
    rows = img_dev * (patches // 2)
    mask_dev = MASK_IMG * img_dev
    group = LANES // dp_count
    scalars = jnp.concatenate([counts, dp_index.astype(jnp.int32)[None]])
    dev_ends = jnp.cumsum(jnp.sum(counts.reshape(dp_count, img_dev), axis=1))
    first_rows = (
        jnp.concatenate([jnp.zeros((1,), jnp.int32), dev_ends[:-1]]) - dp_index + dp_count - 1
    ) // dp_count
    bounds = jnp.concatenate([first_rows, jnp.full((1,), mask_dev)]).astype(jnp.int32)

    xs, zs, zt, inv = prep(scalars, student_rows, teacher_rows, mask_order, dp_count)
    center_row = center[None, :]
    part, ws, wt = sums(
        scalars, zs, zt, student_proto, teacher_proto, center_row, rows, dp_count, True
    )
    everyone = lax.all_to_all(
        jnp.broadcast_to(part[None], (proto_count,) + part.shape), "proto", 0, 0, tiled=True
    )
    totals = jnp.sum(everyone, axis=0)
    cross = totals[2] * (1.0 / STUDENT_TEMP)
    totals = jnp.where(totals[:2] > 0, totals[:2], 1.0)

    def over_dp(side):
        sides = lax.all_to_all(
            jnp.broadcast_to(side[None], (dp_count,) + side.shape), "dp", 0, 0, tiled=True
        )
        return lax.dynamic_slice_in_dim(
            sides.reshape(dp_count, side.shape[0], -1, dp_count, group), dp_index, 1, axis=3
        ).reshape(dp_count, side.shape[0], -1)

    sides = over_dp(jnp.stack([inv, jnp.log(totals[0]) - cross / totals[1]]))
    inv_all, loss_all = sides[:, 0], sides[:, 1]
    near = rows // 2
    chunks = ((near, rows - near, rows * 3 // 8), (0, near, near))
    pieces = []
    for first, count, size in chunks:
        blocks = slice(first // LANES, (first + count) // LANES)
        part = grads(
            scalars, zs, zt, xs, totals[:, blocks], ws, wt, center_row, first, count, size, dp_count
        )
        wire = part.astype(WIRE)
        share = count // dp_count // proto_count
        got = lax.all_to_all(
            wire.reshape(dp_count * proto_count, share, width), ("dp", "proto"), 0, 0, tiled=True
        )
        summed = jnp.sum(
            got.reshape(dp_count, proto_count, share, width).astype(F32), axis=1
        ) * (1.0 / WIRE_GAIN)
        scale = lax.dynamic_slice_in_dim(
            inv_all, first // dp_count + proto_index * share, share, axis=1
        )
        dx = (summed * scale[..., None]).astype(BF16)
        gathered = lax.all_to_all(
            jnp.broadcast_to(dx[None], (proto_count,) + dx.shape), "proto", 0, 0, tiled=True
        )
        pieces.append(gathered.transpose(1, 0, 2, 3).reshape(dp_count, count // dp_count, width))
    student_grad = place(bounds, pieces[::-1], mask_dev)

    position = jnp.arange(mask_dev, dtype=jnp.int32)
    source = jnp.sum((position[:, None] >= first_rows[None, :]).astype(jnp.int32), axis=1) - 1
    index = source * (rows // dp_count) + position - jnp.take(first_rows, source)
    row_loss = jnp.take(loss_all.reshape(-1), index)
    return (row_loss[None, :], student_grad)


def solution(mesh):
    placed = (
        P("dp", None, None),
        P("dp", None, None),
        P(None, "proto"),
        P(None, "proto"),
        P("proto"),
        P(),
        P("dp", None),
    )
    return jax.shard_map(
        local,
        mesh=mesh,
        in_specs=placed,
        out_specs=(P("dp", None), P("dp", None, None)),
        check_vma=False,
    )
```

```python
import functools
import math

import jax
import jax.numpy as jnp
from jax import lax
from jax.experimental import pallas as pl
from jax.experimental.pallas import tpu as pltpu
from jax.sharding import PartitionSpec as P


MASK_IMG = 96
STUDENT_TEMP = 0.1
TEACHER_TEMP = 0.07
EPSILON = 1e-06
LOG2E = math.log2(math.e)
STUDENT_GAIN = LOG2E / STUDENT_TEMP
TEACHER_GAIN = LOG2E / TEACHER_TEMP
WIRE_GAIN = 1024.0
LANES = 128
COL_TILE = 256
PASS1_COLS = 1024
PASS2_COLS = 1024
VMEM_BYTES = 60 * 1024 * 1024
F32 = jnp.float32
BF16 = jnp.bfloat16
WIRE = jnp.float16


def params():
    return pltpu.CompilerParams(
        dimension_semantics=("arbitrary",), vmem_limit_bytes=VMEM_BYTES
    )


def whole(shape):
    return pl.BlockSpec(shape, lambda i, *_: (0,) * len(shape))


def own_sum(scalars, limit):
    return lax.fori_loop(0, limit, lambda i, total: total + scalars[i], jnp.int32(0))


def prep_kernel(
    dp_count, scalars, student, teacher, order, xs_out, zs_out, zt_out, inv_out, xs_all, xt_all, fill
):
    step = pl.program_id(0)
    each, patches = student.shape[:2]
    images = pl.num_programs(0) * each
    most = patches // 2
    first_image = scalars[images * dp_count] * images

    @pl.when(step == 0)
    def _():
        xs_all[...] = jnp.zeros_like(xs_all)
        xt_all[...] = jnp.zeros_like(xt_all)
        fill[0] = 0

    lane = lax.broadcasted_iota(jnp.int32, (8, patches), 1)
    patch = lax.broadcasted_iota(jnp.int32, (most + 16, patches), 1).astype(F32)
    start = fill[0]
    for own in range(each):
        image = step * each + own
        count = scalars[first_image + image]
        base = pl.multiple_of(lax.div(start, 8) * 8, 8)
        listed = jnp.broadcast_to(order[pl.ds(image, 1), :], (8, patches))
        listed = pltpu.roll(jnp.where(lane < count, listed, -1), lax.rem(start, 8), 1)
        column = listed.astype(F32).T[: most + 16, 0:1]
        chosen = jnp.where(patch == jnp.broadcast_to(column, patch.shape), 1.0, 0.0).astype(BF16)
        for rows, kept in ((student, xs_all), (teacher, xt_all)):
            picked = jnp.dot(chosen, rows[own], preferred_element_type=F32)
            for half in range(kept.shape[0]):
                kept[half, pl.ds(base, most + 8), :] += picked[
                    : most + 8, half * LANES : (half + 1) * LANES
                ]
        start += count
    fill[0] = start

    @pl.when(step == pl.num_programs(0) - 1)
    def _():
        phase = lax.rem(own_sum(scalars, first_image), dp_count)
        group = LANES // dp_count
        used = images * most
        for out in (zs_out, zt_out):
            out[used:, :] = jnp.zeros((out.shape[0] - used, out.shape[1]), out.dtype)

        @pl.loop(0, used // LANES)
        def _(block):
            first = block * LANES
            norms = []
            for rank in range(dp_count):
                lead = lax.rem(rank + dp_count - phase, dp_count)
                rows = pl.ds(first + lead, group, stride=dp_count)
                out = pl.ds(pl.multiple_of(first + rank * group, group), group)
                halves = range(xs_all.shape[0])
                student_in = jnp.concatenate([xs_all[h, rows, :] for h in halves], axis=1)
                teacher_in = jnp.concatenate([xt_all[h, rows, :] for h in halves], axis=1)
                student_norm = jnp.sqrt(
                    jnp.sum(student_in * student_in, axis=1, keepdims=True) + EPSILON
                )
                teacher_norm = jnp.sqrt(
                    jnp.sum(teacher_in * teacher_in, axis=1, keepdims=True) + EPSILON
                )
                xs_out[out, :] = student_in.astype(BF16)
                zs_out[out, :] = (student_in / student_norm).astype(BF16)
                zt_out[out, :] = (teacher_in / teacher_norm).astype(BF16)
                norms.append(1.0 / student_norm)
            column = jnp.concatenate(norms, axis=0)
            inv_out[pl.ds(block, 1), :] = jnp.broadcast_to(column, (LANES, LANES)).T[0:1, :]


def prep(scalars, student_rows, teacher_rows, mask_order, dp_count):
    images, patches, width = student_rows.shape
    rows = images * (patches // 2)
    padded = rows + rows // 4
    each = math.gcd(images, 4)
    image_block = pl.BlockSpec((each, patches, width), lambda i, *_: (i, 0, 0))
    return pl.pallas_call(
        functools.partial(prep_kernel, dp_count),
        out_shape=[
            jax.ShapeDtypeStruct((rows, width), BF16),
            jax.ShapeDtypeStruct((padded, width), BF16),
            jax.ShapeDtypeStruct((padded, width), BF16),
            jax.ShapeDtypeStruct((rows // LANES, LANES), F32),
        ],
        grid_spec=pltpu.PrefetchScalarGridSpec(
            num_scalar_prefetch=1,
            grid=(images // each,),
            in_specs=[image_block, image_block, whole(mask_order.shape)],
            out_specs=[
                whole((rows, width)),
                whole((padded, width)),
                whole((padded, width)),
                whole((rows // LANES, LANES)),
            ],
            scratch_shapes=[pltpu.VMEM((width // LANES, rows + patches // 2, LANES), F32)] * 2
            + [pltpu.SMEM((1,), jnp.int32)],
        ),
        compiler_params=params(),
        name="prep",
    )(scalars, student_rows, teacher_rows, mask_order)


def unit_columns(block):
    wide = block.astype(F32)
    return (wide * (1.0 / jnp.sqrt(jnp.sum(wide * wide, axis=0, keepdims=True) + EPSILON))).astype(
        BF16
    )


def row_blocks(scalars, dp_count, first, size, most):
    images = (scalars.shape[0] - 1) // dp_count
    start = scalars[images * dp_count] * images
    used = lax.fori_loop(
        0, images, lambda i, total: total + scalars[start + i], jnp.int32(0)
    )
    used = lax.div(used + (LANES - 1), LANES) * LANES
    return jnp.clip(lax.div(used - first + (size - 1), size), 1, most)


def rows_at(size, block):
    return pl.ds(pl.multiple_of(block * size, size), size)


def round_up(rows, size):
    return (rows + size - 1) // size * size


def sums_kernel(dp_count, first_row, size, raw, scalars, zs, zt, student, teacher, center, *refs):
    if raw:
        sums_out, ws, wt, es_acc, et_acc, cross_acc, s_held, t_held = refs
    else:
        sums_out, es_acc, et_acc, cross_acc, s_held, t_held = refs
        ws, wt = student, teacher
    step, last = pl.program_id(0), pl.num_programs(0) - 1
    cols = ws.shape[1]
    blocks = row_blocks(scalars, dp_count, first_row, size, es_acc.shape[0] // size)

    @pl.when(step == 0)
    def _():
        es_acc[...] = jnp.zeros_like(es_acc)
        et_acc[...] = jnp.zeros_like(et_acc)
        cross_acc[...] = jnp.zeros_like(cross_acc)
        s_held[...] = jnp.full_like(s_held, -1e30)
        t_held[...] = jnp.full_like(t_held, -1e30)

    if raw:

        @pl.when(step < last)
        def _():
            ws[...] = unit_columns(student[...])
            wt[...] = unit_columns(teacher[...])

    def body(block, carry):
        before = jnp.where(block == 0, blocks - 1, block - 1)
        col = jnp.maximum(jnp.where(block == 0, step - 1, step), 0)
        first = pl.multiple_of(before * size, size)
        for tile in range(0, cols, COL_TILE):
            shifts = center[:, pl.ds(pl.multiple_of(col * cols + tile, COL_TILE), COL_TILE)] * TEACHER_GAIN
            for sub in range(0, size, size):
                at = pl.ds(first + sub, size)
                here = slice(sub, sub + size)
                es_sum, et_sum, cross = es_acc[at, :], et_acc[at, :], cross_acc[at, :]
                for c in range(tile, tile + COL_TILE, LANES):
                    shift = shifts[:, c - tile : c - tile + LANES]
                    s = s_held[here, c : c + LANES]
                    es_sum += jnp.exp2(s * STUDENT_GAIN)
                    et = jnp.exp2(t_held[here, c : c + LANES] * TEACHER_GAIN - shift)
                    et_sum += et
                    cross += et * s
                es_acc[at, :], et_acc[at, :], cross_acc[at, :] = es_sum, et_sum, cross
        s_held[...] = jnp.dot(zs[rows_at(size, block), :], ws[...], preferred_element_type=F32)
        t_held[...] = jnp.dot(zt[rows_at(size, block), :], wt[...], preferred_element_type=F32)
        return carry

    lax.fori_loop(0, jnp.where(step == last, 1, blocks), body, 0)

    @pl.when(step == last)
    def _():
        for k, acc in enumerate((es_acc, et_acc, cross_acc)):
            for block in range(sums_out.shape[1]):
                tile = acc[block * LANES : (block + 1) * LANES, :].T
                sums_out[k, block : block + 1, :] = jnp.sum(tile, axis=0, keepdims=True)


def sums(scalars, zs, zt, student, teacher, center, first_row, rows, size, dp_count, raw):
    width, protos = student.shape
    padded = round_up(rows, size)
    part = pl.BlockSpec((pl.Element(padded), pl.Element(width)), lambda i, *_: (first_row, 0))
    cols = min(PASS1_COLS, protos)
    steps = protos // cols
    col_block = pl.BlockSpec((width, cols), lambda i, *_: (0, jnp.minimum(i, steps - 1)))
    outs = [jax.ShapeDtypeStruct((3, rows // LANES, LANES), F32)]
    specs = [whole((3, rows // LANES, LANES))]
    if raw:
        outs += [jax.ShapeDtypeStruct((width, protos), BF16)] * 2
        specs += [col_block] * 2
    out = pl.pallas_call(
        functools.partial(sums_kernel, dp_count, first_row, size, raw),
        out_shape=outs,
        grid_spec=pltpu.PrefetchScalarGridSpec(
            num_scalar_prefetch=1,
            grid=(steps + 1,),
            in_specs=[
                part,
                part,
                col_block,
                col_block,
                whole((1, protos)),
            ],
            out_specs=specs,
            scratch_shapes=[pltpu.VMEM((padded, LANES), F32)] * 3
            + [pltpu.VMEM((size, cols), F32)] * 2,
        ),
        compiler_params=params(),
        cost_estimate=pl.CostEstimate(
            flops=4 * rows * width * protos,
            bytes_accessed=8 * width * protos,
            transcendentals=2 * rows * protos,
        ),
    )(scalars, zs, zt, student, teacher, center)
    return out if raw else (out[0], student, teacher)


def grad_kernel(
    dp_count,
    first_row,
    size,
    first_step,
    scalars,
    zs,
    zt,
    xs,
    totals,
    ws_before,
    ws,
    wt,
    center,
    out,
    es_gain,
    et_gain,
    dz_acc,
    s_held,
    t_held,
):
    step, last = pl.program_id(0), pl.num_programs(0) - 1
    rows = out.shape[0] * out.shape[1]
    cols = ws.shape[1]
    blocks = row_blocks(scalars, dp_count, first_row, size, dz_acc.shape[0] // size)

    @pl.when(step == 0)
    def _():
        dz_acc[...] = jnp.zeros_like(dz_acc)
        s_held[...] = jnp.full_like(s_held, -1e30)
        t_held[...] = jnp.full_like(t_held, -1e30)
        for k, gain in enumerate((es_gain, et_gain)):
            for block in range(rows // LANES):
                line = (1.0 / STUDENT_TEMP) / totals[k, block : block + 1, :]
                gain[block * LANES : (block + 1) * LANES, :] = jnp.broadcast_to(
                    line, (LANES, LANES)
                ).T

    def consume(half, col, slot, columns):
        at = rows_at(size // 2, half)
        es_scale, et_scale = es_gain[at, :], et_gain[at, :]
        shifts = center[:, pl.ds(pl.multiple_of((first_step + col) * cols, cols), cols)] * TEACHER_GAIN
        parts = []
        for c in range(0, cols, LANES):
            s = s_held[slot, :, c : c + LANES]
            es = jnp.exp2(s * STUDENT_GAIN) * es_scale
            et = (
                jnp.exp2(t_held[slot, :, c : c + LANES] * TEACHER_GAIN - shifts[:, c : c + LANES])
                * et_scale
            )
            parts.append((es - et).astype(BF16))
        dz_acc[at, :] += lax.dot_general(
            jnp.concatenate(parts, axis=1),
            columns[...],
            (((1,), (1,)), ((), ())),
            preferred_element_type=F32,
        )

    def produce(half, slot):
        s_held[slot] = jnp.dot(zs[rows_at(size // 2, half), :], ws[...], preferred_element_type=F32)
        t_held[slot] = jnp.dot(zt[rows_at(size // 2, half), :], wt[...], preferred_element_type=F32)

    def turn(block, half_before, col_before, columns_before):
        produce(2 * block, 0)
        consume(half_before, col_before, 1, columns_before)
        produce(2 * block + 1, 1)
        consume(2 * block, step, 0, ws)

    def body(block, carry):
        turn(block, 2 * block - 1, step, ws)
        return carry

    col_before = jnp.maximum(step - 1, 0)

    @pl.when(step < last)
    def _():
        turn(0, 2 * blocks - 1, col_before, ws_before)
        lax.fori_loop(1, blocks, body, 0)

    @pl.when(step == last)
    def _():
        consume(2 * blocks - 1, col_before, 1, ws_before)

    @pl.when(step == last)
    def _():
        group = LANES // dp_count
        for block in range(rows // LANES):
            at = slice(block * LANES, (block + 1) * LANES)
            x = xs[at, :].astype(F32)
            dz = dz_acc[at, :]
            square = jnp.sum(x * x, axis=1, keepdims=True) + EPSILON
            inner = jnp.sum(x * dz, axis=1, keepdims=True)
            part = (dz - x * (inner / square)) * WIRE_GAIN
            for rank in range(dp_count):
                out[rank, block * group : (block + 1) * group, :] = part[
                    rank * group : (rank + 1) * group, :
                ].astype(out.dtype)


def grads(scalars, zs, zt, xs, totals, ws, wt, center, first_row, rows, size, piece, dp_count):
    width, protos = ws.shape
    padded = round_up(rows, size)
    part = lambda count, cols: pl.BlockSpec(
        (pl.Element(count), pl.Element(cols)), lambda i, *_: (first_row, 0)
    )
    cols = min(PASS2_COLS, protos)
    steps = protos // cols // piece[1]
    first_step = piece[0] * steps
    col_block = pl.BlockSpec(
        (width, cols), lambda i, *_: (0, first_step + jnp.minimum(i, steps - 1))
    )
    return pl.pallas_call(
        functools.partial(grad_kernel, dp_count, first_row, size, first_step),
        out_shape=jax.ShapeDtypeStruct((dp_count, rows // dp_count, width), F32),
        grid_spec=pltpu.PrefetchScalarGridSpec(
            num_scalar_prefetch=1,
            grid=(steps + 1,),
            in_specs=[
                part(padded, width),
                part(padded, width),
                part(rows, width),
                whole(totals.shape),
                pl.BlockSpec((width, cols), lambda i, *_: (0, first_step + jnp.maximum(i - 1, 0))),
                col_block,
                col_block,
                whole((1, protos)),
            ],
            out_specs=whole((dp_count, rows // dp_count, width)),
            scratch_shapes=[pltpu.VMEM((padded, LANES), F32)] * 2
            + [pltpu.VMEM((padded, width), F32)]
            + [pltpu.VMEM((2, size // 2, cols), F32)] * 2,
        ),
        compiler_params=params(),
        cost_estimate=pl.CostEstimate(
            flops=6 * rows * width * protos // piece[1],
            bytes_accessed=4 * width * protos // piece[1],
            transcendentals=2 * rows * protos // piece[1],
        ),
    )(scalars, zs, zt, xs, totals, ws, ws, wt, center)


def place_kernel(scalars, *refs):
    *pieces, losses, out, loss_out, stage = refs
    mask_dev, longest = out.shape[1], losses.shape[1]
    lane = lax.broadcasted_iota(jnp.int32, (8, mask_dev), 1)
    placed = jnp.zeros((8, mask_dev), F32)
    for source in range(losses.shape[0]):
        line = jnp.concatenate(
            [
                jnp.broadcast_to(losses[source : source + 1, :], (8, longest)),
                jnp.zeros((8, mask_dev - longest), F32),
            ],
            axis=1,
        )
        inside = (lane >= scalars[source]) & (lane < scalars[source + 1])
        placed = jnp.where(inside, pltpu.roll(line, scalars[source], 1), placed)
    loss_out[...] = placed[0:1, :]
    sources = pieces[0].shape[0]
    stage[...] = jnp.zeros_like(stage)
    to = lax.broadcasted_iota(jnp.int32, (LANES + 8, LANES), 0)
    of = lax.broadcasted_iota(jnp.int32, (LANES + 8, LANES), 1)
    for source in range(sources):
        offset, left = scalars[source], scalars[source + 1] - scalars[source]
        base, shift = pl.multiple_of(offset // 8 * 8, 8), lax.rem(offset, 8)
        done = 0
        for piece in pieces:
            for at in range(0, piece.shape[1], LANES):
                length = min(LANES, piece.shape[1] - at)
                moved = (to[: length + 8, :length] == of[: length + 8, :length] + shift) & (
                    of[: length + 8, :length] < left - done
                )

                @pl.when(left > done)
                def _():
                    stage[pl.ds(base + done, length + 8), :] += jnp.dot(
                        jnp.where(moved, 1.0, 0.0).astype(BF16),
                        piece[source, at : at + length, :],
                        preferred_element_type=F32,
                    )

                done += length
    out[0] = stage[0 : out.shape[1], :].astype(out.dtype)


def place(scalars, pieces, losses, mask_dev):
    width = pieces[0].shape[2]
    return pl.pallas_call(
        place_kernel,
        out_shape=[
            jax.ShapeDtypeStruct((1, mask_dev, width), BF16),
            jax.ShapeDtypeStruct((1, mask_dev), F32),
        ],
        grid_spec=pltpu.PrefetchScalarGridSpec(
            num_scalar_prefetch=1,
            grid=(1,),
            in_specs=[whole(p.shape) for p in pieces] + [whole(losses.shape)],
            out_specs=[whole((1, mask_dev, width)), whole((1, mask_dev))],
            scratch_shapes=[pltpu.VMEM((mask_dev + LANES + 8, width), F32)],
        ),
        compiler_params=params(),
        name="place",
    )(scalars, *pieces, losses)


def local(student_rows, teacher_rows, student_proto, teacher_proto, center, counts, mask_order):
    img_dev, patches, width = student_rows.shape
    dp_count, proto_count = lax.axis_size("dp"), lax.axis_size("proto")
    dp_index, proto_index = lax.axis_index("dp"), lax.axis_index("proto")
    rows = img_dev * (patches // 2)
    mask_dev = MASK_IMG * img_dev
    group = LANES // dp_count
    scalars = jnp.concatenate([counts, dp_index.astype(jnp.int32)[None]])
    dev_ends = jnp.cumsum(jnp.sum(counts.reshape(dp_count, img_dev), axis=1))
    first_rows = (
        jnp.concatenate([jnp.zeros((1,), jnp.int32), dev_ends[:-1]]) - dp_index + dp_count - 1
    ) // dp_count
    bounds = jnp.concatenate([first_rows, jnp.full((1,), mask_dev)]).astype(jnp.int32)

    xs, zs, zt, inv = prep(scalars, student_rows, teacher_rows, mask_order, dp_count)
    center_row = center[None, :]
    near = rows // 2
    chunks = ((0, near, near, near), (near, rows - near, rows * 3 // 8, rows * 3 // 8))

    def over_proto(values):
        return lax.all_to_all(
            jnp.broadcast_to(values[None], (proto_count,) + values.shape), "proto", 0, 0, tiled=True
        )

    def over_dp(side):
        sides = lax.all_to_all(
            jnp.broadcast_to(side[None], (dp_count,) + side.shape), "dp", 0, 0, tiled=True
        )
        return lax.dynamic_slice_in_dim(
            sides.reshape(dp_count, side.shape[0], -1, dp_count, group), dp_index, 1, axis=3
        ).reshape(dp_count, side.shape[0], -1)

    totals, losses = [], []
    ws, wt, raw = student_proto, teacher_proto, True
    for first, count, size, _ in chunks:
        part, ws, wt = sums(scalars, zs, zt, ws, wt, center_row, first, count, size, dp_count, raw)
        raw = False
        if totals:
            part, totals[-1] = lax.optimization_barrier((part, totals[-1]))
        everyone = over_proto(part)
        total = jnp.sum(everyone, axis=0)
        safe = jnp.where(total[:2] > 0, total[:2], 1e30)
        losses.append(jnp.log(safe[0]) - total[2] * (1.0 / STUDENT_TEMP) / safe[1])
        totals.append(safe)
    sides = over_dp(jnp.stack([inv, jnp.concatenate(losses)]))
    inv_all, loss_all = sides[:, 0], sides[:, 1]

    def to_owner(part, first, count):
        share = count // dp_count // proto_count
        wire = part.astype(WIRE).reshape(dp_count * proto_count, share, width)
        got = lax.all_to_all(wire, ("dp", "proto"), 0, 0, tiled=True)
        summed = jnp.sum(
            got.reshape(dp_count, proto_count, share, width).astype(F32), axis=1
        ) * (1.0 / WIRE_GAIN)
        scale = lax.dynamic_slice_in_dim(
            inv_all, first // dp_count + proto_index * share, share, axis=1
        )
        return (summed * scale[..., None]).astype(BF16)

    def to_all(dx, count):
        return over_proto(dx).transpose(1, 0, 2, 3).reshape(dp_count, count // dp_count, width)

    def gradient(at, rows_in, piece):
        first, count, _, size = chunks[at]
        return grads(
            scalars, rows_in, zt, xs, totals[at], ws, wt, center_row, first, count, size,
            piece, dp_count,
        )

    near_part, inv_all = lax.optimization_barrier((gradient(0, zs, (0, 1)), inv_all))
    near_dx = to_owner(near_part, 0, near)
    far = gradient(1, zs, (0, 2))
    late_zs, near_dx = lax.optimization_barrier((zs, near_dx))
    near_piece = to_all(near_dx, near)
    far = far + gradient(1, late_zs, (1, 2))
    far, near_piece = lax.optimization_barrier((far, near_piece))
    far_piece = to_all(to_owner(far, near, rows - near), rows - near)
    student_grad, row_loss = place(bounds, [near_piece, far_piece], loss_all, mask_dev)
    return (row_loss, student_grad)


def solution(mesh):
    placed = (
        P("dp", None, None),
        P("dp", None, None),
        P(None, "proto"),
        P(None, "proto"),
        P("proto"),
        P(),
        P("dp", None),
    )

    return jax.shard_map(
        local,
        mesh=mesh,
        in_specs=placed,
        out_specs=(P("dp", None), P("dp", None, None)),
        check_vma=False,
    )
```
